256 devices in a mesh: hel: 4 (over z_lo), rad: 64 (over z_hi, y, x, core).
Axes of the slice: x: 4, y: 4, z: 8 (z_hi: 2, z_lo: 4; z = z_hi * 4 + z_lo), core: 2. Of those that a mesh axis runs over, the one named last changes fastest.
Arguments:
- packet: float32 [2, 8, 1024, 8, 1024], P(None, 'hel', 'rad'), may hold values from -6 to 6
- radial_weight: float32 [8, 1024], P(None, 'rad'), may hold values from 0.25 to 1.75
- tile_blocks: float32 [24, 128, 128], replicated, may hold values from -0.1875 to 0.1875
- tile_list: int32 [24, 3], replicated, may hold values from 0 to 7, as said below
- coupling: float32 [8, 1024], replicated, may hold values from 0.1 to 0.5
Outputs:
- advanced: float32 [2, 8, 1024, 8, 1024], P(None, 'hel', 'rad')
The draws below stay inside these ranges and needn't reach their ends.
Inputs may be any that keep to these rules, and one draw needn't show every extreme that they name: `tile_list`: each row is (block row, block column, radial weight index): block indices lie below 8 and weight indices below 8; every block row and every weight index occurs in some row; rows may repeat pairs.
All inputs are finite; a program needn't handle non-finite values.
Results may differ from the reference program's by a relative error of at most 0.0001.
Values sent between devices are 32-bit elements; how exact they have to be, the bound alone decides.
A program may use at most 128 MiB of HBM per device.

```python
import jax
import jax.numpy as jnp
from jax import lax

K = 8
V = 8
R = 1024
C = 1024
TILE = 128
NT = 24
Q = 8
TAYLOR = 3


def draw_tile_list(key, part):
    key_rows, key_cols, key_weights, key_pick_rows, key_pick_weights = jax.random.split(jax.random.fold_in(key, 17), 5)
    block_count = C // TILE
    rows_drawn = jax.random.randint(key_rows, (NT,), 0, block_count)
    chosen_rows = jax.random.permutation(key_pick_rows, NT)[:block_count]
    rows_drawn = rows_drawn.at[chosen_rows].set(jnp.arange(block_count, dtype=jnp.int32))
    cols_drawn = jax.random.randint(key_cols, (NT,), 0, block_count)
    weights_drawn = jax.random.randint(key_weights, (NT,), 0, Q)
    chosen_weights = jax.random.permutation(key_pick_weights, NT)[:Q]
    weights_drawn = weights_drawn.at[chosen_weights].set(jnp.arange(Q, dtype=jnp.int32))
    return jnp.stack([rows_drawn, cols_drawn, weights_drawn], axis=1).astype(jnp.int32)


def block_levels(own_key, extent, cuts, smallest, top_value):
    loudness = 1.0
    for axis_at, shards_of in cuts:
        draws = jax.random.uniform(jax.random.fold_in(jax.random.fold_in(own_key, 6), axis_at), (shards_of,), jnp.float32, smallest / len(cuts), top_value / len(cuts))
        loudness = loudness * jnp.repeat(jnp.exp(draws), extent[axis_at] // shards_of).reshape((-1,) + (1,) * (len(extent) - 1 - axis_at))
    return loudness


def scatter_about(own_key, extent, width, reach, pieces=(), kind=jnp.bfloat16):
    entries = jax.random.normal(own_key, extent, jnp.float32) * width
    if len(pieces) > 0:
        entries = block_levels(own_key, extent, pieces, -0.22, 0.18) * entries
    return jnp.clip(entries, min=-reach, max=reach).astype(kind)


def setup_inputs(seed: int = 0) -> dict:
    key_list = jax.random.split(jax.random.key(seed), 6)
    packet = scatter_about(key_list[0], (2, K, R, V, C), 1.0, 6.0, ((1, 4), (2, 64)), jnp.float32)
    radial_weight = jnp.clip(0.25 + 1.5 * jax.random.uniform(key_list[1], (Q, R), jnp.float32) ** block_levels(key_list[1], (Q, R), ((1, 64),), -0.2, 0.2), 0.25, 1.75)
    tile_blocks = scatter_about(key_list[2], (NT, TILE, TILE), (3 * TILE * NT * TILE // C) ** -0.5, 0.1875, (), jnp.float32)
    tile_list = draw_tile_list(jax.random.fold_in(key_list[5], 71), 0)
    coupling = jnp.clip(jax.random.uniform(key_list[4], (K, C), jnp.float32, 0.1, 0.5), 0.1, 0.5)
    return {"packet": packet, "radial_weight": radial_weight, "tile_blocks": tile_blocks, "tile_list": tile_list, "coupling": coupling}


kinetic_scale = 0.5


def potential(term, radial_weight, tile_blocks, tile_list):
    term_shape = term.shape
    blocks = term.reshape(term_shape[0], term_shape[1], term_shape[2], term_shape[3], term_shape[4] // TILE, TILE)

    def add_tile(position, summed):
        target = tile_list[position, 0]
        source = tile_list[position, 1]
        weight_row = tile_list[position, 2]
        source_block = lax.dynamic_index_in_dim(blocks, source, 4, keepdims=False)
        matrix = lax.dynamic_index_in_dim(tile_blocks, position, 0, keepdims=False)
        product = jnp.einsum("ckrvi,ij->ckrvj", source_block, matrix, precision=lax.Precision.HIGHEST)
        factor = lax.dynamic_index_in_dim(radial_weight, weight_row, 0, keepdims=False)
        product = product * factor[None, None, :, None, None]
        current = lax.dynamic_index_in_dim(summed, target, 4, keepdims=False)
        return lax.dynamic_update_index_in_dim(summed, current + product, target, 4)

    summed = lax.fori_loop(0, tile_list.shape[0], add_tile, jnp.zeros(blocks.shape, jnp.float32))
    return summed.reshape(term_shape)


def coriolis(term, coupling, radial_factor):
    helices = term.shape[1]
    padded = jnp.pad(term, ((0, 0), (1, 1), (0, 0), (0, 0), (0, 0)))
    coupled = jnp.concatenate([jnp.zeros((1, coupling.shape[1]), jnp.float32), coupling], axis=0)
    lower = coupled[:helices]
    upper = coupled[1:helices + 1]
    mixed = upper[None, :, None, None, :] * padded[:, 2:] + lower[None, :, None, None, :] * padded[:, :-2]
    return mixed * radial_factor[None, None, :, None, None]


def kinetic(packet):
    wave_index = jnp.arange(R, dtype=jnp.int32)
    signed = jnp.where(wave_index < R // 2, wave_index, wave_index - R).astype(jnp.float32)
    phase_angle = kinetic_scale * (2.0 * jnp.pi * signed / R) ** 2
    complex_field = packet[0] + 1j * packet[1]
    spectrum = jnp.fft.fft(complex_field, axis=1) * jnp.exp(-1j * phase_angle)[None, :, None, None]
    complex_field = jnp.fft.ifft(spectrum, axis=1)
    return jnp.stack([jnp.real(complex_field), jnp.imag(complex_field)]).astype(packet.dtype)


def reference(packet, radial_weight, tile_blocks, tile_list, coupling):
    distance = jnp.arange(R).astype(jnp.float32)
    radial_factor = 1.0 / (1.0 + 3.0 * distance / R) ** 2
    current = kinetic(packet)
    advanced = current
    for degree in range(1, TAYLOR + 1):
        applied = potential(current, radial_weight, tile_blocks, tile_list) + coriolis(current, coupling, radial_factor)
        current = jnp.stack([applied[1], -applied[0]]) / degree
        advanced = advanced + current
    return advanced
```

```python
import functools

import jax
import jax.numpy as jnp
import ml_dtypes
import numpy as np
from jax import lax
from jax.experimental import pallas as pl
from jax.experimental.pallas import tpu as pltpu
from jax.sharding import PartitionSpec as P

R = 1024
HALF = R // 2
TILE = 128
TAYLOR = 3
NT = 24
K = 8
V = 8
CB = 8
Q = 8
MESH = pl.DeviceIdType.MESH
F32 = jnp.float32
BF16 = jnp.bfloat16

kinetic_scale = 0.5


def propagator_tables():
    wave = np.arange(R)
    signed = np.where(wave < R // 2, wave, wave - R).astype(np.float64)
    angle = kinetic_scale * (2.0 * np.pi * signed / R) ** 2
    response = np.fft.ifft(np.exp(-1j * angle))
    shift = np.arange(HALF)[:, None] - np.arange(HALF)[None, :]
    near = response[shift % R]
    far = response[(shift + HALF) % R]
    table = np.zeros((2, 2, HALF // TILE, 2, TILE, HALF), ml_dtypes.bfloat16)
    for i, matrix in enumerate((0.5 * (near + far), 0.5 * (near - far))):
        for c, part in enumerate((matrix.real, matrix.imag)):
            high = part.astype(ml_dtypes.bfloat16)
            low = (part - high.astype(np.float64)).astype(ml_dtypes.bfloat16)
            table[i, 0, :, c] = high.reshape(HALF // TILE, TILE, HALF)
            table[i, 1, :, c] = low.reshape(HALF // TILE, TILE, HALF)
    return table.reshape(2, 2, HALF // TILE, 2 * TILE, HALF)


def split(value):
    high = value.astype(BF16)
    low = (value - high.astype(F32)).astype(BF16)
    return high, low


def take(ref, sem):
    pltpu.make_async_copy(ref, ref, sem).wait()


def kernel(
    x_ref, weight_ref, tiles_ref, list_ref, coupling_ref, table_ref, out_ref,
    xin, send1, recv1a, recv1b, ub, table, ya, yb, recv2a, recv2b,
    tiles, tile_rhs, lhs, sums, adv, rwx, rwb, cpl, send3a, send3b, recv3a, recv3b, res,
    rank, order, src, wrow, same, last,
    xsem, ksem, tsem, ssem1, rsem1, ssem2, rsem2, ssem3, rsem3, wsem, osem,
):
    recv1, yy, recv2 = (recv1a, recv1b), (ya, yb), (recv2a, recv2b)
    send3, recv3 = (send3a, send3b), (recv3a, recv3b)
    zlo = lax.axis_index("hel")
    rad = lax.axis_index("rad")
    core = rad % 2
    x = (rad // 2) % 4
    y = (rad // 8) % 4
    zhi = rad // 32
    z = zhi * 4 + zlo
    q0 = rad % 32
    kap = (x + y) % 4
    cb0 = y * 2 + core

    for p in range(2):
        for part in range(2):
            i = part * 2 + p
            for cb in range(CB):
                pltpu.make_async_copy(
                    x_ref.at[i, :, pl.ds(cb * TILE, TILE)], xin.at[i, cb], xsem.at[i]
                ).start()
    table_copy = pltpu.make_async_copy(table_ref, table, ksem)
    tiles_copy = pltpu.make_async_copy(tiles_ref, tiles, tsem)

    barrier = pltpu.get_barrier_semaphore()

    @pl.loop(0, 64)
    def _(i):
        r = (rad + i) % 64

        @pl.when(jnp.logical_or(r != rad, kap != zlo))
        def _():
            pl.semaphore_signal(barrier, 1, device_id=(kap, r), device_id_type=MESH)

    @pl.loop(1, 8)
    def _(i):
        zz = (z + i) % 8
        pl.semaphore_signal(
            barrier, 1, device_id=(zz % 4, zz // 4 * 32 + q0), device_id_type=MESH
        )

    @pl.loop(1, 32)
    def _(i):
        q = (rad + i) % 32
        pl.semaphore_signal(barrier, 1, device_id=(zlo, zhi * 32 + q), device_id_type=MESH)

    def pack(p):
        for part in range(2):
            i = part * 2 + p
            take(xin.at[i], xsem.at[i])
            for cb in range(CB):
                for v in range(V):
                    send1[p, v, cb, part] = xin[i, cb, pl.ds(v, 16, stride=8), :]

    def scatter_columns(p):
        @pl.loop(0, 64)
        def _(i):
            v = (z + i + 4) % 8
            cb = (y * 2 + core + i // 8 + i) % 8
            dy = cb // 2
            dx = (zlo - dy + 4) % 4
            hel = v % 4
            r = ((v // 4 * 4 + dy) * 4 + dx) * 2 + cb % 2
            source = send1.at[p, v, cb]
            target = recv1[p].at[:, pl.ds(pl.multiple_of(rad * 16, 16), 16), :]
            own = jnp.logical_and(hel == zlo, r == rad)

            @pl.when(own)
            def _():
                pltpu.make_async_copy(source, target, rsem1.at[p]).start()

            @pl.when(jnp.logical_not(own))
            def _():
                pltpu.make_async_remote_copy(
                    source, target, ssem1.at[p], rsem1.at[p],
                    device_id=(hel, r), device_id_type=MESH,
                ).start()

    pack(0)
    pl.semaphore_wait(barrier, 102 - jnp.where(kap == zlo, 1, 0))
    scatter_columns(0)
    pack(1)
    scatter_columns(1)
    table_copy.start()
    tiles_copy.start()

    rwx[zhi] = jnp.zeros((Q, TILE), F32)
    rwx[zhi, :, 0:16] = weight_ref[...]
    weight_copy = pltpu.make_async_remote_copy(
        rwx.at[zhi], rwx.at[zhi], wsem.at[0], wsem.at[1],
        device_id=(zlo, (1 - zhi) * 32 + q0), device_id_type=MESH,
    )
    weight_copy.start()

    @pl.loop(0, NT)
    def _(t):
        mine = list_ref[t, 0]
        count = jnp.int32(0)
        for other in range(NT):
            theirs = list_ref[other, 0]
            ahead = jnp.where(theirs < mine, 1, 0)
            tied = jnp.where(theirs == mine, jnp.where(other < t, 1, 0), 0)
            count = count + ahead + tied
        rank[t] = count

    @pl.loop(0, NT)
    def _(position):
        tile = jnp.int32(0)
        for t in range(NT):
            tile = tile + jnp.where(rank[t] == position, t, 0)
        order[position] = tile
        src[position] = list_ref[tile, 1]
        wrow[position] = list_ref[tile, 2]
        before = order[jnp.maximum(position - 1, 0)]
        same[position] = jnp.where(
            list_ref[tile, 0] == list_ref[before, 0], jnp.where(position > 0, 1, 0), 0
        )

    @pl.loop(0, CB)
    def _(i):
        count = jnp.int32(0)
        for t in range(NT):
            count = count + jnp.where(list_ref[t, 0] <= i, 1, 0)
        last[i] = count

    for cb in range(CB):
        cpl[cb] = coupling_ref[:, cb * TILE:(cb + 1) * TILE]
    sums[0] = jnp.zeros((256, TILE), F32)
    tiles_copy.wait()

    @pl.loop(0, NT)
    def _(position):
        high, low = split(tiles[order[position]])
        tile_rhs[position, 0:TILE] = high
        tile_rhs[position, TILE:2 * TILE] = high
        tile_rhs[position, 2 * TILE:] = low

    weight_copy.wait()
    eye = (
        lax.broadcasted_iota(jnp.int32, (16, 16), 0) == lax.broadcasted_iota(jnp.int32, (16, 16), 1)
    )
    for half in range(2):
        for w in range(Q):
            row = jnp.broadcast_to(rwx[half, w:w + 1, 0:16], (16, 16))
            column = jnp.sum(jnp.where(eye, row, 0.0), axis=1, keepdims=True)
            spread = jnp.broadcast_to(column, (16, TILE))
            rwb[0, w, half * 8:half * 8 + 8] = spread[:8]
            rwb[1, w, half * 8:half * 8 + 8] = spread[8:]
    table_copy.wait()

    for p in range(2):
        take(recv1[p], rsem1.at[p])

        @pl.loop(0, 8)
        def _(i):
            rows = pl.ds(pl.multiple_of(i * 64, 64), 64)
            rows_far = pl.ds(pl.multiple_of(HALF + i * 64, 64), 64)
            for part in range(2):
                near = recv1[p][part, rows, :]
                far = recv1[p][part, rows_far, :]
                for s, value in enumerate((near + far, near - far)):
                    high, low = split(value)
                    ub[s, 0, rows, part * TILE:(part + 1) * TILE] = high
                    ub[s, 1, rows, part * TILE:(part + 1) * TILE] = low

        @pl.loop(0, HALF // TILE)
        def _(block):
            products = []
            for s in range(2):
                total = jnp.dot(table[s, 0, block], ub[s, 0], preferred_element_type=F32)
                total += jnp.dot(table[s, 1, block], ub[s, 0], preferred_element_type=F32)
                total += jnp.dot(table[s, 0, block], ub[s, 1], preferred_element_type=F32)
                real = total[:TILE, :TILE] - total[TILE:, TILE:]
                imag = total[:TILE, TILE:] + total[TILE:, :TILE]
                products.append((real, imag))
            rows = pl.ds(pl.multiple_of(block * TILE, TILE), TILE)
            for part in range(2):
                yy[p][part, 0, rows, :] = products[0][part] + products[1][part]
                yy[p][part, 1, rows, :] = products[0][part] - products[1][part]

        for j in range(2):
            @pl.loop(0, 32)
            def _(i):
                dx = (x + i + y) % 4
                dy = (y + i // 4 + x * 3) % 4
                dc = (core + i // 16 + x + y) % 2
                q = (dy * 4 + dx) * 2 + dc
                source = yy[p].at[:, :, pl.ds(pl.multiple_of(q * 16 + j * 8, 8), 8), :]
                target = recv2[j].at[cb0, :, kap * 2 + p]

                @pl.when(q == q0)
                def _():
                    pltpu.make_async_copy(source, target, rsem2.at[j]).start()

                @pl.when(q != q0)
                def _():
                    pltpu.make_async_remote_copy(
                        source, target, ssem2.at[p], rsem2.at[j],
                        device_id=(zlo, zhi * 32 + q), device_id_type=MESH,
                    ).start()

    for j in range(2):
        field = recv2[j]
        take(field, rsem2.at[j])
        point = lax.broadcasted_iota(jnp.int32, (16, TILE), 0)
        distance = (
            point // 8 * HALF + point % 8 + (q0 * 16 + j * 8)
        ).astype(F32)
        radial_factor = 1.0 / (1.0 + 3.0 * distance / R) ** 2

        def to_lhs(cb, value):
            high, low = split(value)
            lhs[cb, :, 0:TILE] = high
            lhs[cb, :, TILE:2 * TILE] = low
            lhs[cb, :, 2 * TILE:] = high

        @pl.loop(0, CB)
        def _(cb):
            value = field[cb]
            adv[cb] = value.reshape(256, TILE)
            to_lhs(cb, value.reshape(256, TILE))

        for degree in range(1, TAYLOR + 1):
            @pl.loop(0, NT)
            def _(position):
                product = jnp.dot(
                    lhs[src[position]], tile_rhs[position], preferred_element_type=F32
                )
                scaled = product.reshape(16, 16, TILE) * rwb[j, wrow[position]][None]
                carried = jnp.where(same[position] == 1, sums[position], 0.0)
                sums[position + 1] = scaled.reshape(256, TILE) + carried

            @pl.loop(0, CB)
            def _(cb):
                potential = sums[last[cb]].reshape(2, K, 16, TILE)
                strength = cpl[cb]
                rows = [
                    jnp.broadcast_to(strength[k:k + 1], (16, TILE)) * radial_factor
                    for k in range(K - 1)
                ]
                applied = []
                for part in range(2):
                    w = [field[cb, part, k].reshape(16, TILE) for k in range(K)]
                    for k in range(K):
                        value = potential[part, k]
                        if k + 1 < K:
                            value = value + rows[k] * w[k + 1]
                        if k > 0:
                            value = value + rows[k - 1] * w[k - 1]
                        applied.append(value)
                scale = 1.0 / degree
                term = [a * scale for a in applied[K:]] + [a * -scale for a in applied[:K]]
                if degree < TAYLOR:
                    stacked = jnp.concatenate(term, axis=0)
                    adv[cb] = adv[cb] + stacked
                    to_lhs(cb, stacked)
                    for i in range(2 * K):
                        field[cb, i // K, i % K] = term[i].reshape(2, 8, TILE)
                else:
                    lanes = pl.ds(pl.multiple_of(cb * TILE, TILE), TILE)
                    for i in range(2 * K):
                        part, k = i // K, i % K
                        final = adv[cb, i * 16:(i + 1) * 16] + term[i]
                        for half in range(2):
                            send3[j][half * 4 + k // 2, part, k % 2, :, lanes] = final[
                                half * 8:half * 8 + 8
                            ]

        @pl.loop(0, 8)
        def _(o):
            zz = (z + o * 3 + 4) % 8
            source = send3[j].at[zz]
            target = recv3[j].at[z]

            @pl.when(zz == z)
            def _():
                pltpu.make_async_copy(source, target, rsem3.at[j]).start()

            @pl.when(zz != z)
            def _():
                pltpu.make_async_remote_copy(
                    source, target, ssem3.at[j], rsem3.at[j],
                    device_id=(zz % 4, zz // 4 * 32 + q0), device_id_type=MESH,
                ).start()

    for j in range(2):
        take(recv3[j], rsem3.at[j])
        for i in range(4):
            for cb in range(CB):
                for v in range(V):
                    res[i, cb, pl.ds(j * 64 + v, 8, stride=8), :] = recv3[j][
                        v, i // 2, i % 2, :, cb * TILE:(cb + 1) * TILE
                    ]
                pltpu.make_async_copy(
                    res.at[i, cb, pl.ds(j * 64, 64), :],
                    out_ref.at[i, pl.ds(j * 64, 64), pl.ds(cb * TILE, TILE)],
                    osem,
                ).start()

    take(res, osem)
    for p in range(2):
        @pl.when(kap == zlo)
        def _():
            take(send1.at[p, pl.ds(0, 7)], ssem1.at[p])
            take(send1.at[p, 7, pl.ds(0, 7)], ssem1.at[p])

        @pl.when(kap != zlo)
        def _():
            take(send1.at[p], ssem1.at[p])

        take(yy[p].at[:, :, pl.ds(0, HALF - 16), :], ssem2.at[p])
        take(send3[p].at[pl.ds(0, 7)], ssem3.at[p])


def step(packet, radial_weight, tile_blocks, tile_list, coupling):
    flat = packet.reshape(4, 16 * V, CB * TILE)
    table = jnp.asarray(propagator_tables())
    anywhere = pl.BlockSpec(memory_space=pl.ANY)
    vmem = pl.BlockSpec(memory_space=pltpu.VMEM)
    dma = pltpu.SemaphoreType.DMA
    out = pl.pallas_call(
        kernel,
        out_shape=jax.ShapeDtypeStruct(flat.shape, F32),
        in_specs=[
            anywhere, vmem, anywhere, pl.BlockSpec(memory_space=pltpu.SMEM), vmem, anywhere,
        ],
        out_specs=anywhere,
        scratch_shapes=[
            pltpu.VMEM((4, CB, 128, TILE), F32),
            pltpu.VMEM((2, V, CB, 2, 16, TILE), F32),
            pltpu.VMEM((2, R, TILE), F32),
            pltpu.VMEM((2, R, TILE), F32),
            pltpu.VMEM((2, 2, HALF, 2 * TILE), BF16),
            pltpu.VMEM(table.shape, BF16),
            pltpu.VMEM((2, 2, HALF, TILE), F32),
            pltpu.VMEM((2, 2, HALF, TILE), F32),
            pltpu.VMEM((CB, 2, K, 2, 8, TILE), F32),
            pltpu.VMEM((CB, 2, K, 2, 8, TILE), F32),
            pltpu.VMEM((NT, TILE, TILE), F32),
            pltpu.VMEM((NT, 3 * TILE, TILE), BF16),
            pltpu.VMEM((CB, 256, 3 * TILE), BF16),
            pltpu.VMEM((NT + 1, 256, TILE), F32),
            pltpu.VMEM((CB, 256, TILE), F32),
            pltpu.VMEM((2, Q, TILE), F32),
            pltpu.VMEM((2, Q, 16, TILE), F32),
            pltpu.VMEM((CB, K, TILE), F32),
            pltpu.VMEM((8, 2, 2, 8, CB * TILE), F32),
            pltpu.VMEM((8, 2, 2, 8, CB * TILE), F32),
            pltpu.VMEM((8, 2, 2, 8, CB * TILE), F32),
            pltpu.VMEM((8, 2, 2, 8, CB * TILE), F32),
            pltpu.VMEM((4, CB, 128, TILE), F32),
            pltpu.SMEM((NT,), jnp.int32),
            pltpu.SMEM((NT,), jnp.int32),
            pltpu.SMEM((NT,), jnp.int32),
            pltpu.SMEM((NT,), jnp.int32),
            pltpu.SMEM((NT,), jnp.int32),
            pltpu.SMEM((CB,), jnp.int32),
            dma((4,)), dma(()), dma(()),
            dma((2,)), dma((2,)), dma((2,)), dma((2,)), dma((2,)), dma((2,)), dma((2,)), dma(()),
        ],
        compiler_params=pltpu.CompilerParams(
            collective_id=0, has_side_effects=True, vmem_limit_bytes=56 << 20
        ),
        name="wavepacket_step",
    )(flat, radial_weight, tile_blocks, tile_list, coupling, table)
    return out.reshape(packet.shape)


def solution(mesh):
    in_specs = (P(None, "hel", "rad"), P(None, "rad"), P(), P(), P())
    return jax.shard_map(
        step,
        mesh=mesh,
        in_specs=in_specs,
        out_specs=P(None, "hel", "rad"),
        check_vma=False,
    )
```

```python
import functools

import jax
import jax.numpy as jnp
import ml_dtypes
import numpy as np
from jax import lax
from jax.experimental import pallas as pl
from jax.experimental.pallas import tpu as pltpu
from jax.sharding import PartitionSpec as P

R = 1024
HALF = R // 2
TILE = 128
TAYLOR = 3
NT = 24
K = 8
V = 8
CB = 8
Q = 8
MESH = pl.DeviceIdType.MESH
F32 = jnp.float32
BF16 = jnp.bfloat16

kinetic_scale = 0.5


def propagator_tables():
    wave = np.arange(R)
    signed = np.where(wave < R // 2, wave, wave - R).astype(np.float64)
    angle = kinetic_scale * (2.0 * np.pi * signed / R) ** 2
    response = np.fft.ifft(np.exp(-1j * angle))
    shift = np.arange(HALF)[:, None] - np.arange(HALF)[None, :]
    near = response[shift % R]
    far = response[(shift + HALF) % R]
    table = np.zeros((2, 2, HALF // TILE, 2, TILE, HALF), ml_dtypes.bfloat16)
    for i, matrix in enumerate((0.5 * (near + far), 0.5 * (near - far))):
        for c, part in enumerate((matrix.real, matrix.imag)):
            high = part.astype(ml_dtypes.bfloat16)
            low = (part - high.astype(np.float64)).astype(ml_dtypes.bfloat16)
            table[i, 0, :, c] = high.reshape(HALF // TILE, TILE, HALF)
            table[i, 1, :, c] = low.reshape(HALF // TILE, TILE, HALF)
    return table.reshape(2, 2, HALF // TILE, 2 * TILE, HALF)


def split(value):
    high = value.astype(BF16)
    low = (value - high.astype(F32)).astype(BF16)
    return high, low


def take(ref, sem):
    pltpu.make_async_copy(ref, ref, sem).wait()


def kernel(
    x_ref, weight_ref, tiles_ref, list_ref, coupling_ref, table_ref, out_ref,
    xin, send1, recv1a, recv1b, ub, table, ya, yb, recv2a, recv2b,
    tiles, tile_rhs, lhs, sums, adv, rwx, rwb, cpl, send3a, send3b, recv3a, recv3b, res,
    rank, order, src, wrow, same, last,
    xsem, ksem, tsem, ssem1, rsem1, ssem2, rsem2, ssem3, rsem3, wsem, osem,
):
    recv1, yy, recv2 = (recv1a, recv1b), (ya, yb), (recv2a, recv2b)
    send3, recv3 = (send3a, send3b), (recv3a, recv3b)
    zlo = lax.axis_index("hel")
    rad = lax.axis_index("rad")
    core = rad % 2
    x = (rad // 2) % 4
    y = (rad // 8) % 4
    zhi = rad // 32
    z = zhi * 4 + zlo
    q0 = rad % 32
    kap = (x + y) % 4
    cb0 = y * 2 + core

    for p in range(2):
        for part in range(2):
            i = part * 2 + p
            for cb in range(CB):
                pltpu.make_async_copy(
                    x_ref.at[i, :, pl.ds(cb * TILE, TILE)], xin.at[i, cb], xsem.at[i]
                ).start()
    table_copy = pltpu.make_async_copy(table_ref, table, ksem)
    tiles_copy = pltpu.make_async_copy(tiles_ref, tiles, tsem)

    barrier = pltpu.get_barrier_semaphore()

    @pl.loop(0, 64)
    def _(i):
        r = (rad + i) % 64

        @pl.when(jnp.logical_or(r != rad, kap != zlo))
        def _():
            pl.semaphore_signal(barrier, 1, device_id=(kap, r), device_id_type=MESH)

    @pl.loop(1, 8)
    def _(i):
        zz = (z + i) % 8
        pl.semaphore_signal(
            barrier, 1, device_id=(zz % 4, zz // 4 * 32 + q0), device_id_type=MESH
        )

    @pl.loop(1, 32)
    def _(i):
        q = (rad + i) % 32
        pl.semaphore_signal(barrier, 1, device_id=(zlo, zhi * 32 + q), device_id_type=MESH)

    def pack(p):
        for part in range(2):
            i = part * 2 + p
            take(xin.at[i], xsem.at[i])
            for cb in range(CB):
                for v in range(V):
                    send1[p, v, cb, part] = xin[i, cb, pl.ds(v, 16, stride=8), :]

    def scatter_columns(p, h):
        @pl.loop(h * 32, h * 32 + 32)
        def _(i):
            v = (z + i + 4) % 8
            cb = (y * 2 + core + i // 8 + i) % 8
            dy = cb // 2
            dx = (zlo - dy + 4) % 4
            hel = v % 4
            r = ((v // 4 * 4 + dy) * 4 + dx) * 2 + cb % 2
            source = send1.at[p, v, cb]
            target = recv1[p].at[:, pl.ds(pl.multiple_of(rad * 16, 16), 16), :]
            own = jnp.logical_and(hel == zlo, r == rad)

            @pl.when(own)
            def _():
                pltpu.make_async_copy(source, target, rsem1.at[p]).start()

            @pl.when(jnp.logical_not(own))
            def _():
                pltpu.make_async_remote_copy(
                    source, target, ssem1.at[2 * p + h], rsem1.at[p],
                    device_id=(hel, r), device_id_type=MESH,
                ).start()

    def scattered(p, h):
        if h == 0:
            take(send1.at[p, pl.ds(0, 4)], ssem1.at[2 * p])
            return

        @pl.when(kap == zlo)
        def _():
            take(send1.at[p, pl.ds(0, 3)], ssem1.at[2 * p + 1])
            take(send1.at[p, 3, pl.ds(0, 7)], ssem1.at[2 * p + 1])

        @pl.when(kap != zlo)
        def _():
            take(send1.at[p, pl.ds(0, 4)], ssem1.at[2 * p + 1])

    pack(0)
    pl.semaphore_wait(barrier, 102 - jnp.where(kap == zlo, 1, 0))
    scatter_columns(0, 0)
    scatter_columns(0, 1)
    pack(1)
    table_copy.start()
    tiles_copy.start()

    rwx[zhi] = jnp.zeros((Q, TILE), F32)
    rwx[zhi, :, 0:16] = weight_ref[...]
    weight_copy = pltpu.make_async_remote_copy(
        rwx.at[zhi], rwx.at[zhi], wsem.at[0], wsem.at[1],
        device_id=(zlo, (1 - zhi) * 32 + q0), device_id_type=MESH,
    )
    weight_copy.start()

    scattered(0, 0)
    scatter_columns(1, 0)
    scattered(0, 1)
    scatter_columns(1, 1)

    @pl.loop(0, NT)
    def _(t):
        mine = list_ref[0, t]
        count = jnp.int32(0)
        for other in range(NT):
            theirs = list_ref[0, other]
            ahead = jnp.where(theirs < mine, 1, 0)
            tied = jnp.where(theirs == mine, jnp.where(other < t, 1, 0), 0)
            count = count + ahead + tied
        rank[t] = count

    @pl.loop(0, NT)
    def _(position):
        tile = jnp.int32(0)
        for t in range(NT):
            tile = tile + jnp.where(rank[t] == position, t, 0)
        order[position] = tile
        src[position] = list_ref[1, tile]
        wrow[position] = list_ref[2, tile]
        before = order[jnp.maximum(position - 1, 0)]
        same[position] = jnp.where(
            list_ref[0, tile] == list_ref[0, before], jnp.where(position > 0, 1, 0), 0
        )

    @pl.loop(0, CB)
    def _(i):
        count = jnp.int32(0)
        for t in range(NT):
            count = count + jnp.where(list_ref[0, t] <= i, 1, 0)
        last[i] = count

    for cb in range(CB):
        cpl[cb] = coupling_ref[:, cb * TILE:(cb + 1) * TILE]
    sums[0] = jnp.zeros((256, TILE), F32)
    tiles_copy.wait()

    @pl.loop(0, NT)
    def _(position):
        high, low = split(tiles[order[position]])
        tile_rhs[position, 0:TILE] = high
        tile_rhs[position, TILE:2 * TILE] = high
        tile_rhs[position, 2 * TILE:] = low

    weight_copy.wait()
    eye = (
        lax.broadcasted_iota(jnp.int32, (16, 16), 0) == lax.broadcasted_iota(jnp.int32, (16, 16), 1)
    )
    for half in range(2):
        for w in range(Q):
            row = jnp.broadcast_to(rwx[half, w:w + 1, 0:16], (16, 16))
            column = jnp.sum(jnp.where(eye, row, 0.0), axis=1, keepdims=True)
            spread = jnp.broadcast_to(column, (16, TILE))
            rwb[0, w, half * 8:half * 8 + 8] = spread[:8]
            rwb[1, w, half * 8:half * 8 + 8] = spread[8:]
    table_copy.wait()

    for p in range(2):
        take(recv1[p], rsem1.at[p])

        @pl.loop(0, 8)
        def _(i):
            rows = pl.ds(pl.multiple_of(i * 64, 64), 64)
            rows_far = pl.ds(pl.multiple_of(HALF + i * 64, 64), 64)
            for part in range(2):
                near = recv1[p][part, rows, :]
                far = recv1[p][part, rows_far, :]
                for s, value in enumerate((near + far, near - far)):
                    high, low = split(value)
                    ub[s, 0, rows, part * TILE:(part + 1) * TILE] = high
                    ub[s, 1, rows, part * TILE:(part + 1) * TILE] = low

        @pl.loop(0, HALF // TILE)
        def _(block):
            products = []
            for s in range(2):
                total = jnp.dot(table[s, 0, block], ub[s, 0], preferred_element_type=F32)
                total += jnp.dot(table[s, 1, block], ub[s, 0], preferred_element_type=F32)
                total += jnp.dot(table[s, 0, block], ub[s, 1], preferred_element_type=F32)
                real = total[:TILE, :TILE] - total[TILE:, TILE:]
                imag = total[:TILE, TILE:] + total[TILE:, :TILE]
                products.append((real, imag))
            rows = pl.ds(pl.multiple_of(block * TILE, TILE), TILE)
            for part in range(2):
                yy[p][part, 0, rows, :] = products[0][part] + products[1][part]
                yy[p][part, 1, rows, :] = products[0][part] - products[1][part]

        for j in range(2):
            @pl.loop(0, 32)
            def _(i):
                dx = (x + i + y) % 4
                dy = (y + i // 4 + x * 3) % 4
                dc = (core + i // 16 + x + y) % 2
                q = (dy * 4 + dx) * 2 + dc
                source = yy[p].at[:, :, pl.ds(pl.multiple_of(q * 16 + j * 8, 8), 8), :]
                target = recv2[j].at[cb0, :, kap * 2 + p]

                @pl.when(q == q0)
                def _():
                    pltpu.make_async_copy(source, target, rsem2.at[j]).start()

                @pl.when(q != q0)
                def _():
                    pltpu.make_async_remote_copy(
                        source, target, ssem2.at[p], rsem2.at[j],
                        device_id=(zlo, zhi * 32 + q), device_id_type=MESH,
                    ).start()

    for j in range(2):
        field = recv2[j]
        take(field, rsem2.at[j])
        point = lax.broadcasted_iota(jnp.int32, (16, TILE), 0)
        distance = (
            point // 8 * HALF + point % 8 + (q0 * 16 + j * 8)
        ).astype(F32)
        radial_factor = 1.0 / (1.0 + 3.0 * distance / R) ** 2

        def to_lhs(cb, value):
            high, low = split(value)
            lhs[cb, :, 0:TILE] = high
            lhs[cb, :, TILE:2 * TILE] = low
            lhs[cb, :, 2 * TILE:] = high

        @pl.loop(0, CB)
        def _(cb):
            value = field[cb]
            adv[cb] = value.reshape(256, TILE)
            to_lhs(cb, value.reshape(256, TILE))

        for degree in range(1, TAYLOR + 1):
            @pl.loop(0, NT, unroll=NT)
            def _(position):
                product = jnp.dot(
                    lhs[src[position]], tile_rhs[position], preferred_element_type=F32
                )
                scaled = product.reshape(16, 16, TILE) * rwb[j, wrow[position]][None]
                carried = jnp.where(same[position] == 1, sums[position], 0.0)
                sums[position + 1] = scaled.reshape(256, TILE) + carried

            @pl.loop(0, CB)
            def _(cb):
                potential = sums[last[cb]].reshape(2, K, 16, TILE)
                strength = cpl[cb]
                rows = [
                    jnp.broadcast_to(strength[k:k + 1], (16, TILE)) * radial_factor
                    for k in range(K - 1)
                ]
                applied = []
                for part in range(2):
                    w = [field[cb, part, k].reshape(16, TILE) for k in range(K)]
                    for k in range(K):
                        value = potential[part, k]
                        if k + 1 < K:
                            value = value + rows[k] * w[k + 1]
                        if k > 0:
                            value = value + rows[k - 1] * w[k - 1]
                        applied.append(value)
                scale = 1.0 / degree
                term = [a * scale for a in applied[K:]] + [a * -scale for a in applied[:K]]
                if degree < TAYLOR:
                    stacked = jnp.concatenate(term, axis=0)
                    adv[cb] = adv[cb] + stacked
                    to_lhs(cb, stacked)
                    for i in range(2 * K):
                        field[cb, i // K, i % K] = term[i].reshape(2, 8, TILE)
                else:
                    lanes = pl.ds(pl.multiple_of(cb * TILE, TILE), TILE)
                    for i in range(2 * K):
                        part, k = i // K, i % K
                        final = adv[cb, i * 16:(i + 1) * 16] + term[i]
                        for half in range(2):
                            send3[j][half * 4 + k // 2, part, k % 2, :, lanes] = final[
                                half * 8:half * 8 + 8
                            ]

        @pl.loop(0, 8)
        def _(o):
            zz = (z + o * 3 + 4) % 8
            source = send3[j].at[zz]
            target = recv3[j].at[z]

            @pl.when(zz == z)
            def _():
                pltpu.make_async_copy(source, target, rsem3.at[j]).start()

            @pl.when(zz != z)
            def _():
                pltpu.make_async_remote_copy(
                    source, target, ssem3.at[j], rsem3.at[j],
                    device_id=(zz % 4, zz // 4 * 32 + q0), device_id_type=MESH,
                ).start()

    for j in range(2):
        take(recv3[j], rsem3.at[j])
        for i in range(4):
            for cb in range(CB):
                for v in range(V):
                    res[i, cb, pl.ds(j * 64 + v, 8, stride=8), :] = recv3[j][
                        v, i // 2, i % 2, :, cb * TILE:(cb + 1) * TILE
                    ]
                pltpu.make_async_copy(
                    res.at[i, cb, pl.ds(j * 64, 64), :],
                    out_ref.at[i, pl.ds(j * 64, 64), pl.ds(cb * TILE, TILE)],
                    osem,
                ).start()

    take(res, osem)
    scattered(1, 0)
    scattered(1, 1)
    for p in range(2):
        take(yy[p].at[:, :, pl.ds(0, HALF - 16), :], ssem2.at[p])
        take(send3[p].at[pl.ds(0, 7)], ssem3.at[p])


def step(packet, radial_weight, tile_blocks, tile_list, coupling):
    flat = packet.reshape(4, 16 * V, CB * TILE)
    table = jnp.asarray(propagator_tables())
    anywhere = pl.BlockSpec(memory_space=pl.ANY)
    vmem = pl.BlockSpec(memory_space=pltpu.VMEM)
    dma = pltpu.SemaphoreType.DMA
    out = pl.pallas_call(
        kernel,
        out_shape=jax.ShapeDtypeStruct(flat.shape, F32),
        in_specs=[
            anywhere, vmem, anywhere, pl.BlockSpec(memory_space=pltpu.SMEM), vmem, anywhere,
        ],
        out_specs=anywhere,
        scratch_shapes=[
            pltpu.VMEM((4, CB, 128, TILE), F32),
            pltpu.VMEM((2, V, CB, 2, 16, TILE), F32),
            pltpu.VMEM((2, R, TILE), F32),
            pltpu.VMEM((2, R, TILE), F32),
            pltpu.VMEM((2, 2, HALF, 2 * TILE), BF16),
            pltpu.VMEM(table.shape, BF16),
            pltpu.VMEM((2, 2, HALF, TILE), F32),
            pltpu.VMEM((2, 2, HALF, TILE), F32),
            pltpu.VMEM((CB, 2, K, 2, 8, TILE), F32),
            pltpu.VMEM((CB, 2, K, 2, 8, TILE), F32),
            pltpu.VMEM((NT, TILE, TILE), F32),
            pltpu.VMEM((NT, 3 * TILE, TILE), BF16),
            pltpu.VMEM((CB, 256, 3 * TILE), BF16),
            pltpu.VMEM((NT + 1, 256, TILE), F32),
            pltpu.VMEM((CB, 256, TILE), F32),
            pltpu.VMEM((2, Q, TILE), F32),
            pltpu.VMEM((2, Q, 16, TILE), F32),
            pltpu.VMEM((CB, K, TILE), F32),
            pltpu.VMEM((8, 2, 2, 8, CB * TILE), F32),
            pltpu.VMEM((8, 2, 2, 8, CB * TILE), F32),
            pltpu.VMEM((8, 2, 2, 8, CB * TILE), F32),
            pltpu.VMEM((8, 2, 2, 8, CB * TILE), F32),
            pltpu.VMEM((4, CB, 128, TILE), F32),
            pltpu.SMEM((NT,), jnp.int32),
            pltpu.SMEM((NT,), jnp.int32),
            pltpu.SMEM((NT,), jnp.int32),
            pltpu.SMEM((NT,), jnp.int32),
            pltpu.SMEM((NT,), jnp.int32),
            pltpu.SMEM((CB,), jnp.int32),
            dma((4,)), dma(()), dma(()),
            dma((4,)), dma((2,)), dma((2,)), dma((2,)), dma((2,)), dma((2,)), dma((2,)), dma(()),
        ],
        compiler_params=pltpu.CompilerParams(
            collective_id=0, has_side_effects=True, vmem_limit_bytes=56 << 20
        ),
        name="wavepacket_step",
    )(flat, radial_weight, tile_blocks, tile_list.T, coupling, table)
    return out.reshape(packet.shape)


def solution(mesh):
    in_specs = (P(None, "hel", "rad"), P(None, "rad"), P(), P(), P())
    return jax.shard_map(
        step,
        mesh=mesh,
        in_specs=in_specs,
        out_specs=P(None, "hel", "rad"),
        check_vma=False,
    )
```

```python
import functools

import jax
import jax.numpy as jnp
import ml_dtypes
import numpy as np
from jax import lax
from jax.experimental import pallas as pl
from jax.experimental.pallas import tpu as pltpu
from jax.sharding import PartitionSpec as P

R = 1024
HALF = R // 2
TILE = 128
TAYLOR = 3
NT = 24
K = 8
V = 8
CB = 8
Q = 8
MESH = pl.DeviceIdType.MESH
F32 = jnp.float32
BF16 = jnp.bfloat16

kinetic_scale = 0.5


def propagator_tables():
    wave = np.arange(R)
    signed = np.where(wave < R // 2, wave, wave - R).astype(np.float64)
    angle = kinetic_scale * (2.0 * np.pi * signed / R) ** 2
    response = np.fft.ifft(np.exp(-1j * angle))
    rows = np.arange(HALF).reshape(32, 2, 8).transpose(1, 0, 2).reshape(HALF)
    shift = rows[:, None] - np.arange(HALF)[None, :]
    near = response[shift % R]
    far = response[(shift + HALF) % R]
    table = np.zeros((2, 2, HALF // TILE, 2, TILE, HALF), ml_dtypes.bfloat16)
    for i, matrix in enumerate((0.5 * (near + far), 0.5 * (near - far))):
        for c, part in enumerate((matrix.real, matrix.imag)):
            high = part.astype(ml_dtypes.bfloat16)
            low = (part - high.astype(np.float64)).astype(ml_dtypes.bfloat16)
            table[i, 0, :, c] = high.reshape(HALF // TILE, TILE, HALF)
            table[i, 1, :, c] = low.reshape(HALF // TILE, TILE, HALF)
    return table.reshape(2, 2, HALF // TILE, 2 * TILE, HALF)


def split(value):
    high = value.astype(BF16)
    low = (value - high.astype(F32)).astype(BF16)
    return high, low


def take(ref, sem):
    pltpu.make_async_copy(ref, ref, sem).wait()


def kernel(
    x_ref, weight_ref, tiles_ref, list_ref, coupling_ref, table_ref, out_ref,
    xin, send1, recv1a, recv1b, ub, table, ya, yb, recv2,
    tiles, tile_rhs, lhs, sums, adv, rwx, rwb, cpl, send3, recv3a, recv3b, res,
    rank, order, src, wrow, same, last,
    xsem, ksem, tsem, ssem1, rsem1, ssem2, rsem2, ssem3, rsem3, wsem, osem,
):
    recv1, yy, recv3 = (recv1a, recv1b), (ya, yb), (recv3a, recv3b)
    zlo = lax.axis_index("hel")
    rad = lax.axis_index("rad")
    core = rad % 2
    x = (rad // 2) % 4
    y = (rad // 8) % 4
    zhi = rad // 32
    z = zhi * 4 + zlo
    q0 = rad % 32
    kap = (x + y) % 4
    cb0 = y * 2 + core

    for p in range(2):
        for part in range(2):
            i = part * 2 + p
            for cb in range(CB):
                pltpu.make_async_copy(
                    x_ref.at[i, :, pl.ds(cb * TILE, TILE)], xin.at[i, cb], xsem.at[i]
                ).start()
    table_copy = pltpu.make_async_copy(table_ref, table, ksem)
    tiles_copy = pltpu.make_async_copy(tiles_ref, tiles, tsem)

    barrier = pltpu.get_barrier_semaphore()

    @pl.loop(0, 64)
    def _(i):
        r = (rad + i) % 64

        @pl.when(jnp.logical_or(r != rad, kap != zlo))
        def _():
            pl.semaphore_signal(barrier, 1, device_id=(kap, r), device_id_type=MESH)

    @pl.loop(1, 8)
    def _(i):
        zz = (z + i) % 8
        pl.semaphore_signal(
            barrier, 1, device_id=(zz % 4, zz // 4 * 32 + q0), device_id_type=MESH
        )

    @pl.loop(1, 32)
    def _(i):
        q = (rad + i) % 32
        pl.semaphore_signal(barrier, 1, device_id=(zlo, zhi * 32 + q), device_id_type=MESH)

    def pack(p):
        for part in range(2):
            i = part * 2 + p
            take(xin.at[i], xsem.at[i])
            for cb in range(CB):
                for v in range(V):
                    send1[p, v, cb, part] = xin[i, cb, pl.ds(v, 16, stride=8), :]

    def scatter_columns(p, h):
        @pl.loop(h * 32, h * 32 + 32)
        def _(i):
            v = (z + i + 4) % 8
            cb = (y * 2 + core + i // 8 + i) % 8
            dy = cb // 2
            dx = (zlo - dy + 4) % 4
            hel = v % 4
            r = ((v // 4 * 4 + dy) * 4 + dx) * 2 + cb % 2
            source = send1.at[p, v, cb]
            target = recv1[p].at[:, pl.ds(pl.multiple_of(rad * 16, 16), 16), :]
            own = jnp.logical_and(hel == zlo, r == rad)

            @pl.when(own)
            def _():
                pltpu.make_async_copy(source, target, rsem1.at[p]).start()

            @pl.when(jnp.logical_not(own))
            def _():
                pltpu.make_async_remote_copy(
                    source, target, ssem1.at[2 * p + h], rsem1.at[p],
                    device_id=(hel, r), device_id_type=MESH,
                ).start()

    def scattered(p, h):
        if h == 0:
            take(send1.at[p, pl.ds(0, 4)], ssem1.at[2 * p])
            return

        @pl.when(kap == zlo)
        def _():
            take(send1.at[p, pl.ds(0, 3)], ssem1.at[2 * p + 1])
            take(send1.at[p, 3, pl.ds(0, 7)], ssem1.at[2 * p + 1])

        @pl.when(kap != zlo)
        def _():
            take(send1.at[p, pl.ds(0, 4)], ssem1.at[2 * p + 1])

    pack(0)
    pl.semaphore_wait(barrier, 102 - jnp.where(kap == zlo, 1, 0))
    scatter_columns(0, 0)
    scatter_columns(0, 1)
    pack(1)
    table_copy.start()
    tiles_copy.start()

    rwx[zhi] = jnp.zeros((Q, TILE), F32)
    rwx[zhi, :, 0:16] = weight_ref[...]
    weight_copy = pltpu.make_async_remote_copy(
        rwx.at[zhi], rwx.at[zhi], wsem.at[0], wsem.at[1],
        device_id=(zlo, (1 - zhi) * 32 + q0), device_id_type=MESH,
    )
    weight_copy.start()

    scattered(0, 0)
    scatter_columns(1, 0)
    scattered(0, 1)
    scatter_columns(1, 1)

    @pl.loop(0, NT)
    def _(t):
        mine = list_ref[0, t]
        count = jnp.int32(0)
        for other in range(NT):
            theirs = list_ref[0, other]
            ahead = jnp.where(theirs < mine, 1, 0)
            tied = jnp.where(theirs == mine, jnp.where(other < t, 1, 0), 0)
            count = count + ahead + tied
        rank[t] = count

    @pl.loop(0, NT)
    def _(position):
        tile = jnp.int32(0)
        for t in range(NT):
            tile = tile + jnp.where(rank[t] == position, t, 0)
        order[position] = tile
        src[position] = list_ref[1, tile]
        wrow[position] = list_ref[2, tile]
        before = order[jnp.maximum(position - 1, 0)]
        same[position] = jnp.where(
            list_ref[0, tile] == list_ref[0, before], jnp.where(position > 0, 1, 0), 0
        )

    @pl.loop(0, CB)
    def _(i):
        count = jnp.int32(0)
        for t in range(NT):
            count = count + jnp.where(list_ref[0, t] <= i, 1, 0)
        last[i] = count

    for cb in range(CB):
        cpl[cb] = coupling_ref[:, cb * TILE:(cb + 1) * TILE]
    sums[0] = jnp.zeros((TILE, TILE), F32)
    tiles_copy.wait()

    @pl.loop(0, NT)
    def _(position):
        high, low = split(tiles[order[position]])
        tile_rhs[position, 0:TILE] = high
        tile_rhs[position, TILE:2 * TILE] = high
        tile_rhs[position, 2 * TILE:] = low

    weight_copy.wait()
    eye = (
        lax.broadcasted_iota(jnp.int32, (16, 16), 0) == lax.broadcasted_iota(jnp.int32, (16, 16), 1)
    )
    for half in range(2):
        for w in range(Q):
            row = jnp.broadcast_to(rwx[half, w:w + 1, 0:16], (16, 16))
            column = jnp.sum(jnp.where(eye, row, 0.0), axis=1, keepdims=True)
            spread = jnp.broadcast_to(column, (16, TILE))
            rwb[half, 0, w] = spread[:8]
            rwb[half, 1, w] = spread[8:]
    table_copy.wait()

    def gather_points(p, c):
        @pl.loop(0, 32)
        def _(i):
            dx = (x + i + y) % 4
            dy = (y + i // 4 + x * 3) % 4
            dc = (core + i // 16 + x + y) % 2
            q = (dy * 4 + dx) * 2 + dc
            rows = pl.ds(pl.multiple_of(q * 8, 8), 8)
            source = yy[p].at[:, (zhi + 1 - c // 2) % 2, c % 2, rows, :]
            target = recv2.at[c, cb0, :, kap * 2 + p]

            @pl.when(q == q0)
            def _():
                pltpu.make_async_copy(source, target, rsem2.at[c]).start()

            @pl.when(q != q0)
            def _():
                pltpu.make_async_remote_copy(
                    source, target, ssem2.at[c if p else 4], rsem2.at[c],
                    device_id=(zlo, zhi * 32 + q), device_id_type=MESH,
                ).start()

    for p in range(2):
        take(recv1[p], rsem1.at[p])

        @pl.loop(0, 8)
        def _(i):
            rows = pl.ds(pl.multiple_of(i * 64, 64), 64)
            rows_far = pl.ds(pl.multiple_of(HALF + i * 64, 64), 64)
            for part in range(2):
                near = recv1[p][part, rows, :]
                far = recv1[p][part, rows_far, :]
                for s, value in enumerate((near + far, near - far)):
                    high, low = split(value)
                    ub[s, 0, rows, part * TILE:(part + 1) * TILE] = high
                    ub[s, 1, rows, part * TILE:(part + 1) * TILE] = low

        for j in range(2):
            @pl.loop(0, 2)
            def _(i):
                block = j * 2 + i
                products = []
                for s in range(2):
                    total = jnp.dot(table[s, 0, block], ub[s, 0], preferred_element_type=F32)
                    total += jnp.dot(table[s, 1, block], ub[s, 0], preferred_element_type=F32)
                    total += jnp.dot(table[s, 0, block], ub[s, 1], preferred_element_type=F32)
                    real = total[:TILE, :TILE] - total[TILE:, TILE:]
                    imag = total[:TILE, TILE:] + total[TILE:, :TILE]
                    products.append((real, imag))
                rows = pl.ds(pl.multiple_of(i * TILE, TILE), TILE)
                for part in range(2):
                    yy[p][part, 0, j, rows, :] = products[0][part] + products[1][part]
                    yy[p][part, 1, j, rows, :] = products[0][part] - products[1][part]

            for c in ((j, j + 2) if p == 0 else (0,) if j == 0 else ()):
                gather_points(p, c)

    @pl.loop(0, 4)
    def _(c):
        half = (zhi + 1 - c // 2) % 2
        j = c % 2
        take(yb.at[:, 0, 0, pl.ds(0, 248), :], ssem2.at[c])

        @pl.when(c < 3)
        def _():
            gather_points(1, c + 1)

        take(recv2.at[c], rsem2.at[c])
        point = lax.broadcasted_iota(jnp.int32, (8, TILE), 0)
        distance = (point + (half * HALF + q0 * 16 + j * 8)).astype(F32)
        radial_factor = 1.0 / (1.0 + 3.0 * distance / R) ** 2

        def to_lhs(cb, value):
            high, low = split(value)
            lhs[cb, :, 0:TILE] = high
            lhs[cb, :, TILE:2 * TILE] = low
            lhs[cb, :, 2 * TILE:] = high

        @pl.loop(0, CB)
        def _(cb):
            value = recv2[c, cb].reshape(TILE, TILE)
            adv[cb] = value
            to_lhs(cb, value)

        for degree in range(1, TAYLOR + 1):
            @pl.loop(0, NT, unroll=NT)
            def _(position):
                product = jnp.dot(
                    lhs[src[position]], tile_rhs[position], preferred_element_type=F32
                )
                scaled = product.reshape(16, 8, TILE) * rwb[half, j, wrow[position]][None]
                carried = jnp.where(same[position] == 1, sums[position], 0.0)
                sums[position + 1] = scaled.reshape(TILE, TILE) + carried

            @pl.loop(0, CB)
            def _(cb):
                potential = sums[last[cb]].reshape(2, K, 8, TILE)
                strength = cpl[cb]
                rows = [
                    jnp.broadcast_to(strength[k:k + 1], (8, TILE)) * radial_factor
                    for k in range(K - 1)
                ]
                applied = []
                for part in range(2):
                    w = [recv2[c, cb, part, k] for k in range(K)]
                    for k in range(K):
                        value = potential[part, k]
                        if k + 1 < K:
                            value = value + rows[k] * w[k + 1]
                        if k > 0:
                            value = value + rows[k - 1] * w[k - 1]
                        applied.append(value)
                scale = 1.0 / degree
                term = [a * scale for a in applied[K:]] + [a * -scale for a in applied[:K]]
                if degree < TAYLOR:
                    stacked = jnp.concatenate(term, axis=0)
                    adv[cb] = adv[cb] + stacked
                    to_lhs(cb, stacked)
                    for i in range(2 * K):
                        recv2[c, cb, i // K, i % K] = term[i]
                else:
                    lanes = pl.ds(pl.multiple_of(cb * TILE, TILE), TILE)
                    for i in range(2 * K):
                        part, k = i // K, i % K
                        send3[c, k // 2, part, k % 2, :, lanes] = adv[cb, i * 8:(i + 1) * 8] + term[i]

        @pl.loop(0, 4)
        def _(o):
            pair = (zlo + o) % 4
            source = send3.at[c, pair]
            for jj in range(2):
                target = recv3[jj].at[z]
                own = jnp.logical_and(pair == zlo, c >= 2)

                @pl.when(jnp.logical_and(own, j == jj))
                def _():
                    pltpu.make_async_copy(source, target, rsem3.at[jj]).start()

                @pl.when(jnp.logical_and(jnp.logical_not(own), j == jj))
                def _():
                    pltpu.make_async_remote_copy(
                        source, target, ssem3.at[c], rsem3.at[jj],
                        device_id=(pair, half * 32 + q0), device_id_type=MESH,
                    ).start()

    for j in range(2):
        take(recv3[j], rsem3.at[j])
        for i in range(4):
            for cb in range(CB):
                for v in range(V):
                    res[i, cb, pl.ds(j * 64 + v, 8, stride=8), :] = recv3[j][
                        v, i // 2, i % 2, :, cb * TILE:(cb + 1) * TILE
                    ]
                pltpu.make_async_copy(
                    res.at[i, cb, pl.ds(j * 64, 64), :],
                    out_ref.at[i, pl.ds(j * 64, 64), pl.ds(cb * TILE, TILE)],
                    osem,
                ).start()

    take(res, osem)
    scattered(1, 0)
    scattered(1, 1)
    take(ya.at[:, :, :, pl.ds(0, 248), :], ssem2.at[4])
    for c in range(4):
        take(send3.at[c, pl.ds(0, 4 if c < 2 else 3)], ssem3.at[c])


def step(packet, radial_weight, tile_blocks, tile_list, coupling):
    flat = packet.reshape(4, 16 * V, CB * TILE)
    table = jnp.asarray(propagator_tables())
    anywhere = pl.BlockSpec(memory_space=pl.ANY)
    vmem = pl.BlockSpec(memory_space=pltpu.VMEM)
    dma = pltpu.SemaphoreType.DMA
    out = pl.pallas_call(
        kernel,
        out_shape=jax.ShapeDtypeStruct(flat.shape, F32),
        in_specs=[
            anywhere, vmem, anywhere, pl.BlockSpec(memory_space=pltpu.SMEM), vmem, anywhere,
        ],
        out_specs=anywhere,
        scratch_shapes=[
            pltpu.VMEM((4, CB, 128, TILE), F32),
            pltpu.VMEM((2, V, CB, 2, 16, TILE), F32),
            pltpu.VMEM((2, R, TILE), F32),
            pltpu.VMEM((2, R, TILE), F32),
            pltpu.VMEM((2, 2, HALF, 2 * TILE), BF16),
            pltpu.VMEM(table.shape, BF16),
            pltpu.VMEM((2, 2, 2, HALF // 2, TILE), F32),
            pltpu.VMEM((2, 2, 2, HALF // 2, TILE), F32),
            pltpu.VMEM((4, CB, 2, K, 8, TILE), F32),
            pltpu.VMEM((NT, TILE, TILE), F32),
            pltpu.VMEM((NT, 3 * TILE, TILE), BF16),
            pltpu.VMEM((CB, TILE, 3 * TILE), BF16),
            pltpu.VMEM((NT + 1, TILE, TILE), F32),
            pltpu.VMEM((CB, TILE, TILE), F32),
            pltpu.VMEM((2, Q, TILE), F32),
            pltpu.VMEM((2, 2, Q, 8, TILE), F32),
            pltpu.VMEM((CB, K, TILE), F32),
            pltpu.VMEM((4, 4, 2, 2, 8, CB * TILE), F32),
            pltpu.VMEM((8, 2, 2, 8, CB * TILE), F32),
            pltpu.VMEM((8, 2, 2, 8, CB * TILE), F32),
            pltpu.VMEM((4, CB, 128, TILE), F32),
            pltpu.SMEM((NT,), jnp.int32),
            pltpu.SMEM((NT,), jnp.int32),
            pltpu.SMEM((NT,), jnp.int32),
            pltpu.SMEM((NT,), jnp.int32),
            pltpu.SMEM((NT,), jnp.int32),
            pltpu.SMEM((CB,), jnp.int32),
            dma((4,)), dma(()), dma(()),
            dma((4,)), dma((2,)), dma((5,)), dma((4,)), dma((4,)), dma((2,)), dma((2,)), dma(()),
        ],
        compiler_params=pltpu.CompilerParams(
            collective_id=0, has_side_effects=True, vmem_limit_bytes=56 << 20
        ),
        name="wavepacket_step",
    )(flat, radial_weight, tile_blocks, tile_list.T, coupling, table)
    return out.reshape(packet.shape)


def solution(mesh):
    in_specs = (P(None, "hel", "rad"), P(None, "rad"), P(), P(), P())
    return jax.shard_map(
        step,
        mesh=mesh,
        in_specs=in_specs,
        out_specs=P(None, "hel", "rad"),
        check_vma=False,
    )
```

```python
import functools

import jax
import jax.numpy as jnp
import ml_dtypes
import numpy as np
from jax import lax
from jax.experimental import pallas as pl
from jax.experimental.pallas import tpu as pltpu
from jax.sharding import PartitionSpec as P

R = 1024
HALF = R // 2
TILE = 128
TAYLOR = 3
NT = 24
K = 8
V = 8
CB = 8
Q = 8
MESH = pl.DeviceIdType.MESH
F32 = jnp.float32
BF16 = jnp.bfloat16

kinetic_scale = 0.5


def propagator_tables():
    wave = np.arange(R)
    signed = np.where(wave < R // 2, wave, wave - R).astype(np.float64)
    angle = kinetic_scale * (2.0 * np.pi * signed / R) ** 2
    response = np.fft.ifft(np.exp(-1j * angle))
    rows = np.arange(HALF).reshape(32, 2, 8).transpose(1, 0, 2).reshape(HALF)
    shift = rows[:, None] - np.arange(HALF)[None, :]
    near = response[shift % R]
    far = response[(shift + HALF) % R]
    table = np.zeros((2, 2, HALF // TILE, 2, TILE, HALF), ml_dtypes.bfloat16)
    for i, matrix in enumerate((0.5 * (near + far), 0.5 * (near - far))):
        for c, part in enumerate((matrix.real, matrix.imag)):
            high = part.astype(ml_dtypes.bfloat16)
            low = (part - high.astype(np.float64)).astype(ml_dtypes.bfloat16)
            table[i, 0, :, c] = high.reshape(HALF // TILE, TILE, HALF)
            table[i, 1, :, c] = low.reshape(HALF // TILE, TILE, HALF)
    return table.reshape(2, 2, HALF // TILE, 2 * TILE, HALF)


def split(value):
    high = value.astype(BF16)
    low = (value - high.astype(F32)).astype(BF16)
    return high, low


def take(ref, sem):
    pltpu.make_async_copy(ref, ref, sem).wait()


def kernel(
    x_ref, weight_ref, tiles_ref, list_ref, coupling_ref, table_ref, out_ref,
    xin, send1, recv1a, recv1b, ub, table, ya, yb, recv2,
    tiles, tile_rhs, lhs, sums, adv, rwx, rwb, cpl, send3, recv3a, recv3b, res,
    rank, order, src, wrow, same, last,
    xsem, ksem, tsem, ssem1, rsem1, ssem2, rsem2, ssem3, rsem3, wsem, osem,
):
    recv1, yy, recv3 = (recv1a, recv1b), (ya, yb), (recv3a, recv3b)
    zlo = lax.axis_index("hel")
    rad = lax.axis_index("rad")
    core = rad % 2
    x = (rad // 2) % 4
    y = (rad // 8) % 4
    zhi = rad // 32
    z = zhi * 4 + zlo
    q0 = rad % 32
    kap = (x + y) % 4
    cb0 = y * 2 + core

    for p in range(2):
        for part in range(2):
            i = part * 2 + p
            for cb in range(CB):
                pltpu.make_async_copy(
                    x_ref.at[i, :, pl.ds(cb * TILE, TILE)], xin.at[i, cb], xsem.at[i]
                ).start()
    table_copy = pltpu.make_async_copy(table_ref, table, ksem)
    tiles_copy = pltpu.make_async_copy(tiles_ref, tiles, tsem)

    barrier = pltpu.get_barrier_semaphore()

    @pl.loop(0, 64)
    def _(i):
        r = (rad + i) % 64

        @pl.when(jnp.logical_or(r != rad, kap != zlo))
        def _():
            pl.semaphore_signal(barrier, 1, device_id=(kap, r), device_id_type=MESH)

    @pl.loop(1, 8)
    def _(i):
        zz = (z + i) % 8
        pl.semaphore_signal(
            barrier, 1, device_id=(zz % 4, zz // 4 * 32 + q0), device_id_type=MESH
        )

    @pl.loop(1, 32)
    def _(i):
        q = (rad + i) % 32
        pl.semaphore_signal(barrier, 1, device_id=(zlo, zhi * 32 + q), device_id_type=MESH)

    def pack(p):
        for part in range(2):
            i = part * 2 + p
            take(xin.at[i], xsem.at[i])
            for cb in range(CB):
                for v in range(V):
                    send1[p, v, cb, part] = xin[i, cb, pl.ds(v, 16, stride=8), :]

    def scatter_columns(p, h):
        @pl.loop(h * 32, h * 32 + 32)
        def _(i):
            v = (z + i * (1 + 6 * core) + 4) % 8
            cb = (y * 2 + core + i // 8 + i) % 8
            dy = cb // 2
            dx = (zlo - dy + 4) % 4
            hel = v % 4
            r = ((v // 4 * 4 + dy) * 4 + dx) * 2 + cb % 2
            source = send1.at[p, v, cb]
            target = recv1[p].at[:, pl.ds(pl.multiple_of(rad * 16, 16), 16), :]
            own = jnp.logical_and(hel == zlo, r == rad)

            @pl.when(own)
            def _():
                pltpu.make_async_copy(source, target, rsem1.at[p]).start()

            @pl.when(jnp.logical_not(own))
            def _():
                pltpu.make_async_remote_copy(
                    source, target, ssem1.at[2 * p + h], rsem1.at[p],
                    device_id=(hel, r), device_id_type=MESH,
                ).start()

    def scattered(p, h):
        if h == 0:
            take(send1.at[p, pl.ds(0, 4)], ssem1.at[2 * p])
            return

        @pl.when(kap == zlo)
        def _():
            take(send1.at[p, pl.ds(0, 3)], ssem1.at[2 * p + 1])
            take(send1.at[p, 3, pl.ds(0, 7)], ssem1.at[2 * p + 1])

        @pl.when(kap != zlo)
        def _():
            take(send1.at[p, pl.ds(0, 4)], ssem1.at[2 * p + 1])

    pack(0)
    pl.semaphore_wait(barrier, 102 - jnp.where(kap == zlo, 1, 0))
    scatter_columns(0, 0)
    scatter_columns(0, 1)
    pack(1)
    table_copy.start()
    tiles_copy.start()

    rwx[zhi] = jnp.zeros((Q, TILE), F32)
    rwx[zhi, :, 0:16] = weight_ref[...]
    weight_copy = pltpu.make_async_remote_copy(
        rwx.at[zhi], rwx.at[zhi], wsem.at[0], wsem.at[1],
        device_id=(zlo, (1 - zhi) * 32 + q0), device_id_type=MESH,
    )
    weight_copy.start()

    scattered(0, 0)
    scatter_columns(1, 0)
    scattered(0, 1)
    scatter_columns(1, 1)

    @pl.loop(0, NT)
    def _(t):
        mine = list_ref[0, t]
        count = jnp.int32(0)
        for other in range(NT):
            theirs = list_ref[0, other]
            ahead = jnp.where(theirs < mine, 1, 0)
            tied = jnp.where(theirs == mine, jnp.where(other < t, 1, 0), 0)
            count = count + ahead + tied
        rank[t] = count

    @pl.loop(0, NT)
    def _(position):
        tile = jnp.int32(0)
        for t in range(NT):
            tile = tile + jnp.where(rank[t] == position, t, 0)
        order[position] = tile
        src[position] = list_ref[1, tile]
        wrow[position] = list_ref[2, tile]
        before = order[jnp.maximum(position - 1, 0)]
        same[position] = jnp.where(
            list_ref[0, tile] == list_ref[0, before], jnp.where(position > 0, 1, 0), 0
        )

    @pl.loop(0, CB)
    def _(i):
        count = jnp.int32(0)
        for t in range(NT):
            count = count + jnp.where(list_ref[0, t] <= i, 1, 0)
        last[i] = count

    for cb in range(CB):
        cpl[cb] = coupling_ref[:, cb * TILE:(cb + 1) * TILE]
    sums[0] = jnp.zeros((TILE, TILE), F32)
    tiles_copy.wait()

    @pl.loop(0, NT)
    def _(position):
        high, low = split(tiles[order[position]])
        tile_rhs[position, 0:TILE] = high
        tile_rhs[position, TILE:2 * TILE] = high
        tile_rhs[position, 2 * TILE:] = low

    weight_copy.wait()
    eye = (
        lax.broadcasted_iota(jnp.int32, (16, 16), 0) == lax.broadcasted_iota(jnp.int32, (16, 16), 1)
    )
    for half in range(2):
        for w in range(Q):
            row = jnp.broadcast_to(rwx[half, w:w + 1, 0:16], (16, 16))
            column = jnp.sum(jnp.where(eye, row, 0.0), axis=1, keepdims=True)
            spread = jnp.broadcast_to(column, (16, TILE))
            rwb[half, 0, w] = spread[:8]
            rwb[half, 1, w] = spread[8:]
    table_copy.wait()

    def gather_points(p, c):
        @pl.loop(0, 32)
        def _(i):
            dx = (x + i + y) % 4
            dy = (y + i // 4 + x * 3) % 4
            dc = (core + i // 16 + x + y) % 2
            q = (dy * 4 + dx) * 2 + dc
            rows = pl.ds(pl.multiple_of(q * 8, 8), 8)
            source = yy[p].at[:, (zhi + 1 - c // 2) % 2, c % 2, rows, :]
            target = recv2.at[c, cb0, :, kap * 2 + p]

            @pl.when(q == q0)
            def _():
                pltpu.make_async_copy(source, target, rsem2.at[c]).start()

            @pl.when(q != q0)
            def _():
                pltpu.make_async_remote_copy(
                    source, target, ssem2.at[c if p else 4], rsem2.at[c],
                    device_id=(zlo, zhi * 32 + q), device_id_type=MESH,
                ).start()

    for p in range(2):
        take(recv1[p], rsem1.at[p])

        @pl.loop(0, 8)
        def _(i):
            rows = pl.ds(pl.multiple_of(i * 64, 64), 64)
            rows_far = pl.ds(pl.multiple_of(HALF + i * 64, 64), 64)
            for part in range(2):
                near = recv1[p][part, rows, :]
                far = recv1[p][part, rows_far, :]
                for s, value in enumerate((near + far, near - far)):
                    high, low = split(value)
                    ub[s, 0, rows, part * TILE:(part + 1) * TILE] = high
                    ub[s, 1, rows, part * TILE:(part + 1) * TILE] = low

        for j in range(2):
            @pl.loop(0, 2)
            def _(i):
                block = j * 2 + i
                products = []
                for s in range(2):
                    total = jnp.dot(table[s, 0, block], ub[s, 0], preferred_element_type=F32)
                    total += jnp.dot(table[s, 1, block], ub[s, 0], preferred_element_type=F32)
                    total += jnp.dot(table[s, 0, block], ub[s, 1], preferred_element_type=F32)
                    real = total[:TILE, :TILE] - total[TILE:, TILE:]
                    imag = total[:TILE, TILE:] + total[TILE:, :TILE]
                    products.append((real, imag))
                rows = pl.ds(pl.multiple_of(i * TILE, TILE), TILE)
                for part in range(2):
                    yy[p][part, 0, j, rows, :] = products[0][part] + products[1][part]
                    yy[p][part, 1, j, rows, :] = products[0][part] - products[1][part]

            for c in ((j, j + 2) if p == 0 else (0,) if j == 0 else ()):
                gather_points(p, c)

    @pl.loop(0, 4)
    def _(c):
        half = (zhi + 1 - c // 2) % 2
        j = c % 2
        take(yb.at[:, 0, 0, pl.ds(0, 248), :], ssem2.at[c])

        @pl.when(c < 3)
        def _():
            gather_points(1, c + 1)

        take(recv2.at[c], rsem2.at[c])
        point = lax.broadcasted_iota(jnp.int32, (8, TILE), 0)
        distance = (point + (half * HALF + q0 * 16 + j * 8)).astype(F32)
        radial_factor = 1.0 / (1.0 + 3.0 * distance / R) ** 2

        def to_lhs(cb, value):
            high, low = split(value)
            lhs[cb, :, 0:TILE] = high
            lhs[cb, :, TILE:2 * TILE] = low
            lhs[cb, :, 2 * TILE:] = high

        @pl.loop(0, CB)
        def _(cb):
            value = recv2[c, cb].reshape(TILE, TILE)
            adv[cb] = value
            to_lhs(cb, value)

        for degree in range(1, TAYLOR + 1):
            @pl.loop(0, NT, unroll=NT)
            def _(position):
                product = jnp.dot(
                    lhs[src[position]], tile_rhs[position], preferred_element_type=F32
                )
                scaled = product.reshape(16, 8, TILE) * rwb[half, j, wrow[position]][None]
                carried = jnp.where(same[position] == 1, sums[position], 0.0)
                sums[position + 1] = scaled.reshape(TILE, TILE) + carried

            @pl.loop(0, CB)
            def _(cb):
                potential = sums[last[cb]].reshape(2, K, 8, TILE)
                strength = cpl[cb]
                rows = [
                    jnp.broadcast_to(strength[k:k + 1], (8, TILE)) * radial_factor
                    for k in range(K - 1)
                ]
                applied = []
                for part in range(2):
                    w = [recv2[c, cb, part, k] for k in range(K)]
                    for k in range(K):
                        value = potential[part, k]
                        if k + 1 < K:
                            value = value + rows[k] * w[k + 1]
                        if k > 0:
                            value = value + rows[k - 1] * w[k - 1]
                        applied.append(value)
                scale = 1.0 / degree
                term = [a * scale for a in applied[K:]] + [a * -scale for a in applied[:K]]
                if degree < TAYLOR:
                    stacked = jnp.concatenate(term, axis=0)
                    adv[cb] = adv[cb] + stacked
                    to_lhs(cb, stacked)
                    for i in range(2 * K):
                        recv2[c, cb, i // K, i % K] = term[i]
                else:
                    lanes = pl.ds(pl.multiple_of(cb * TILE, TILE), TILE)
                    for i in range(2 * K):
                        part, k = i // K, i % K
                        send3[c, k // 2, part, k % 2, :, lanes] = adv[cb, i * 8:(i + 1) * 8] + term[i]

        @pl.loop(0, 4)
        def _(o):
            pair = (zlo + o) % 4
            source = send3.at[c, pair]
            for jj in range(2):
                target = recv3[jj].at[z]
                own = jnp.logical_and(pair == zlo, c >= 2)

                @pl.when(jnp.logical_and(own, j == jj))
                def _():
                    pltpu.make_async_copy(source, target, rsem3.at[jj]).start()

                @pl.when(jnp.logical_and(jnp.logical_not(own), j == jj))
                def _():
                    pltpu.make_async_remote_copy(
                        source, target, ssem3.at[c], rsem3.at[jj],
                        device_id=(pair, half * 32 + q0), device_id_type=MESH,
                    ).start()

    for j in range(2):
        take(recv3[j], rsem3.at[j])
        for i in range(4):
            for cb in range(CB):
                for v in range(V):
                    res[i, cb, pl.ds(j * 64 + v, 8, stride=8), :] = recv3[j][
                        v, i // 2, i % 2, :, cb * TILE:(cb + 1) * TILE
                    ]
                pltpu.make_async_copy(
                    res.at[i, cb, pl.ds(j * 64, 64), :],
                    out_ref.at[i, pl.ds(j * 64, 64), pl.ds(cb * TILE, TILE)],
                    osem,
                ).start()

    take(res, osem)
    scattered(1, 0)
    scattered(1, 1)
    take(ya.at[:, :, :, pl.ds(0, 248), :], ssem2.at[4])
    for c in range(4):
        take(send3.at[c, pl.ds(0, 4 if c < 2 else 3)], ssem3.at[c])


def step(packet, radial_weight, tile_blocks, tile_list, coupling):
    flat = packet.reshape(4, 16 * V, CB * TILE)
    table = jnp.asarray(propagator_tables())
    anywhere = pl.BlockSpec(memory_space=pl.ANY)
    vmem = pl.BlockSpec(memory_space=pltpu.VMEM)
    dma = pltpu.SemaphoreType.DMA
    out = pl.pallas_call(
        kernel,
        out_shape=pltpu.VMEM(flat.shape, F32),
        in_specs=[
            anywhere, vmem, anywhere, pl.BlockSpec(memory_space=pltpu.SMEM), vmem, anywhere,
        ],
        out_specs=vmem,
        scratch_shapes=[
            pltpu.VMEM((4, CB, 128, TILE), F32),
            pltpu.VMEM((2, V, CB, 2, 16, TILE), F32),
            pltpu.VMEM((2, R, TILE), F32),
            pltpu.VMEM((2, R, TILE), F32),
            pltpu.VMEM((2, 2, HALF, 2 * TILE), BF16),
            pltpu.VMEM(table.shape, BF16),
            pltpu.VMEM((2, 2, 2, HALF // 2, TILE), F32),
            pltpu.VMEM((2, 2, 2, HALF // 2, TILE), F32),
            pltpu.VMEM((4, CB, 2, K, 8, TILE), F32),
            pltpu.VMEM((NT, TILE, TILE), F32),
            pltpu.VMEM((NT, 3 * TILE, TILE), BF16),
            pltpu.VMEM((CB, TILE, 3 * TILE), BF16),
            pltpu.VMEM((NT + 1, TILE, TILE), F32),
            pltpu.VMEM((CB, TILE, TILE), F32),
            pltpu.VMEM((2, Q, TILE), F32),
            pltpu.VMEM((2, 2, Q, 8, TILE), F32),
            pltpu.VMEM((CB, K, TILE), F32),
            pltpu.VMEM((4, 4, 2, 2, 8, CB * TILE), F32),
            pltpu.VMEM((8, 2, 2, 8, CB * TILE), F32),
            pltpu.VMEM((8, 2, 2, 8, CB * TILE), F32),
            pltpu.VMEM((4, CB, 128, TILE), F32),
            pltpu.SMEM((NT,), jnp.int32),
            pltpu.SMEM((NT,), jnp.int32),
            pltpu.SMEM((NT,), jnp.int32),
            pltpu.SMEM((NT,), jnp.int32),
            pltpu.SMEM((NT,), jnp.int32),
            pltpu.SMEM((CB,), jnp.int32),
            dma((4,)), dma(()), dma(()),
            dma((4,)), dma((2,)), dma((5,)), dma((4,)), dma((4,)), dma((2,)), dma((2,)), dma(()),
        ],
        compiler_params=pltpu.CompilerParams(
            collective_id=0, has_side_effects=True, vmem_limit_bytes=60 << 20
        ),
        name="wavepacket_step",
    )(flat, radial_weight, tile_blocks, tile_list.T, coupling, table)
    return out.reshape(packet.shape)


def solution(mesh):
    in_specs = (P(None, "hel", "rad"), P(None, "rad"), P(), P(), P())
    return jax.shard_map(
        step,
        mesh=mesh,
        in_specs=in_specs,
        out_specs=P(None, "hel", "rad"),
        check_vma=False,
    )
```

```python
import functools

import jax
import jax.numpy as jnp
import ml_dtypes
import numpy as np
from jax import lax
from jax.experimental import pallas as pl
from jax.experimental.pallas import tpu as pltpu
from jax.sharding import PartitionSpec as P

R = 1024
HALF = R // 2
TILE = 128
TAYLOR = 3
NT = 24
K = 8
V = 8
CB = 8
Q = 8
MESH = pl.DeviceIdType.MESH
F32 = jnp.float32
BF16 = jnp.bfloat16

kinetic_scale = 0.5


def propagator_tables():
    wave = np.arange(R)
    signed = np.where(wave < R // 2, wave, wave - R).astype(np.float64)
    angle = kinetic_scale * (2.0 * np.pi * signed / R) ** 2
    response = np.fft.ifft(np.exp(-1j * angle))
    rows = np.arange(HALF).reshape(32, 2, 8).transpose(1, 0, 2).reshape(HALF)
    shift = rows[:, None] - np.arange(HALF)[None, :]
    near = response[shift % R]
    far = response[(shift + HALF) % R]
    table = np.zeros((2, 2, HALF // TILE, 2, TILE, HALF), ml_dtypes.bfloat16)
    for i, matrix in enumerate((0.5 * (near + far), 0.5 * (near - far))):
        for c, part in enumerate((matrix.real, matrix.imag)):
            high = part.astype(ml_dtypes.bfloat16)
            low = (part - high.astype(np.float64)).astype(ml_dtypes.bfloat16)
            table[i, 0, :, c] = high.reshape(HALF // TILE, TILE, HALF)
            table[i, 1, :, c] = low.reshape(HALF // TILE, TILE, HALF)
    return table.reshape(2, 2, HALF // TILE, 2 * TILE, HALF)


def split(value):
    high = value.astype(BF16)
    low = (value - high.astype(F32)).astype(BF16)
    return high, low


def take(ref, sem):
    pltpu.make_async_copy(ref, ref, sem).wait()


def kernel(
    x_ref, weight_ref, tiles_ref, list_ref, coupling_ref, table_ref, out_ref,
    xin, send1, recv1a, recv1b, ub, table, ya, yb, recv2,
    tiles, tile_rhs, lhs, sums, adv, rwx, rwb, cpl, send3, recv3a, recv3b, res,
    rank, order, src, wrow, same, last,
    xsem, ksem, tsem, ssem1, rsem1, ssem2, rsem2, ssem3, rsem3, wsem, osem,
):
    recv1, yy, recv3 = (recv1a, recv1b), (ya, yb), (recv3a, recv3b)
    zlo = lax.axis_index("hel")
    rad = lax.axis_index("rad")
    core = rad % 2
    x = (rad // 2) % 4
    y = (rad // 8) % 4
    zhi = rad // 32
    z = zhi * 4 + zlo
    q0 = rad % 32
    kap = (x + y) % 4
    cb0 = y * 2 + core

    table_copy = pltpu.make_async_copy(table_ref, table, ksem)
    tiles_copy = pltpu.make_async_copy(tiles_ref, tiles, tsem)

    barrier = pltpu.get_barrier_semaphore()

    @pl.loop(0, 64)
    def _(i):
        r = (rad + i) % 64

        @pl.when(jnp.logical_or(r != rad, kap != zlo))
        def _():
            pl.semaphore_signal(barrier, 1, device_id=(kap, r), device_id_type=MESH)

    for p in range(2):
        for part in range(2):
            i = part * 2 + p
            for cb in range(CB):
                pltpu.make_async_copy(
                    x_ref.at[i, :, pl.ds(cb * TILE, TILE)], xin.at[i, cb], xsem.at[i]
                ).start()

    @pl.loop(1, 8)
    def _(i):
        zz = (z + i) % 8
        pl.semaphore_signal(
            barrier, 1, device_id=(zz % 4, zz // 4 * 32 + q0), device_id_type=MESH
        )

    @pl.loop(1, 32)
    def _(i):
        q = (rad + i) % 32
        pl.semaphore_signal(barrier, 1, device_id=(zlo, zhi * 32 + q), device_id_type=MESH)

    def pack(p):
        for part in range(2):
            i = part * 2 + p
            take(xin.at[i], xsem.at[i])
            for cb in range(CB):
                for v in range(V):
                    send1[p, v, cb, part] = xin[i, cb, pl.ds(v, 16, stride=8), :]

    def scatter_columns(p, h):
        @pl.loop(h * 32, h * 32 + 32)
        def _(i):
            v = (z + i * (1 + 6 * core) + 4) % 8
            cb = (y * 2 + core + i // 8 + i) % 8
            dy = cb // 2
            dx = (zlo - dy + 4) % 4
            hel = v % 4
            r = ((v // 4 * 4 + dy) * 4 + dx) * 2 + cb % 2
            source = send1.at[p, v, cb]
            target = recv1[p].at[:, pl.ds(pl.multiple_of(rad * 16, 16), 16), :]
            own = jnp.logical_and(hel == zlo, r == rad)

            @pl.when(own)
            def _():
                pltpu.make_async_copy(source, target, rsem1.at[p]).start()

            @pl.when(jnp.logical_not(own))
            def _():
                pltpu.make_async_remote_copy(
                    source, target, ssem1.at[2 * p + h], rsem1.at[p],
                    device_id=(hel, r), device_id_type=MESH,
                ).start()

    def scattered(p, h):
        if h == 0:
            take(send1.at[p, pl.ds(0, 4)], ssem1.at[2 * p])
            return

        @pl.when(kap == zlo)
        def _():
            take(send1.at[p, pl.ds(0, 3)], ssem1.at[2 * p + 1])
            take(send1.at[p, 3, pl.ds(0, 7)], ssem1.at[2 * p + 1])

        @pl.when(kap != zlo)
        def _():
            take(send1.at[p, pl.ds(0, 4)], ssem1.at[2 * p + 1])

    pack(0)
    pl.semaphore_wait(barrier, 102 - jnp.where(kap == zlo, 1, 0))
    scatter_columns(0, 0)
    scatter_columns(0, 1)
    pack(1)
    table_copy.start()
    tiles_copy.start()

    rwx[zhi] = jnp.zeros((Q, TILE), F32)
    rwx[zhi, :, 0:16] = weight_ref[...]
    weight_copy = pltpu.make_async_remote_copy(
        rwx.at[zhi], rwx.at[zhi], wsem.at[0], wsem.at[1],
        device_id=(zlo, (1 - zhi) * 32 + q0), device_id_type=MESH,
    )
    weight_copy.start()

    scattered(0, 0)
    scatter_columns(1, 0)
    scattered(0, 1)
    scatter_columns(1, 1)

    @pl.loop(0, NT)
    def _(t):
        mine = list_ref[0, t]
        count = jnp.int32(0)
        for other in range(NT):
            theirs = list_ref[0, other]
            ahead = jnp.where(theirs < mine, 1, 0)
            tied = jnp.where(theirs == mine, jnp.where(other < t, 1, 0), 0)
            count = count + ahead + tied
        rank[t] = count

    @pl.loop(0, NT)
    def _(position):
        tile = jnp.int32(0)
        for t in range(NT):
            tile = tile + jnp.where(rank[t] == position, t, 0)
        order[position] = tile
        src[position] = list_ref[1, tile]
        wrow[position] = list_ref[2, tile]
        before = order[jnp.maximum(position - 1, 0)]
        same[position] = jnp.where(
            list_ref[0, tile] == list_ref[0, before], jnp.where(position > 0, 1, 0), 0
        )

    @pl.loop(0, CB)
    def _(i):
        count = jnp.int32(0)
        for t in range(NT):
            count = count + jnp.where(list_ref[0, t] <= i, 1, 0)
        last[i] = count

    for cb in range(CB):
        cpl[cb] = coupling_ref[:, cb * TILE:(cb + 1) * TILE]
    sums[0] = jnp.zeros((TILE, TILE), F32)
    tiles_copy.wait()

    @pl.loop(0, NT)
    def _(position):
        high, low = split(tiles[order[position]])
        tile_rhs[position, 0:TILE] = high
        tile_rhs[position, TILE:2 * TILE] = high
        tile_rhs[position, 2 * TILE:] = low

    weight_copy.wait()
    eye = (
        lax.broadcasted_iota(jnp.int32, (16, 16), 0) == lax.broadcasted_iota(jnp.int32, (16, 16), 1)
    )
    for half in range(2):
        for w in range(Q):
            row = jnp.broadcast_to(rwx[half, w:w + 1, 0:16], (16, 16))
            column = jnp.sum(jnp.where(eye, row, 0.0), axis=1, keepdims=True)
            spread = jnp.broadcast_to(column, (16, TILE))
            rwb[half, 0, w] = spread[:8]
            rwb[half, 1, w] = spread[8:]
    table_copy.wait()

    def gather_points(p, c):
        @pl.loop(0, 32)
        def _(i):
            dx = (x + i + y) % 4
            dy = (y + i // 4 + x * 3) % 4
            dc = (core + i // 16 + x + y) % 2
            q = (dy * 4 + dx) * 2 + dc
            rows = pl.ds(pl.multiple_of(q * 8, 8), 8)
            source = yy[p].at[:, (zhi + 1 - c // 2) % 2, c % 2, rows, :]
            target = recv2.at[c, cb0, :, kap * 2 + p]

            @pl.when(q == q0)
            def _():
                pltpu.make_async_copy(source, target, rsem2.at[c]).start()

            @pl.when(q != q0)
            def _():
                pltpu.make_async_remote_copy(
                    source, target, ssem2.at[c if p else 4], rsem2.at[c],
                    device_id=(zlo, zhi * 32 + q), device_id_type=MESH,
                ).start()

    for p in range(2):
        take(recv1[p], rsem1.at[p])

        @pl.loop(0, 8)
        def _(i):
            rows = pl.ds(pl.multiple_of(i * 64, 64), 64)
            rows_far = pl.ds(pl.multiple_of(HALF + i * 64, 64), 64)
            for part in range(2):
                near = recv1[p][part, rows, :]
                far = recv1[p][part, rows_far, :]
                for s, value in enumerate((near + far, near - far)):
                    high, low = split(value)
                    ub[s, 0, rows, part * TILE:(part + 1) * TILE] = high
                    ub[s, 1, rows, part * TILE:(part + 1) * TILE] = low

        for j in range(2):
            @pl.loop(0, 2)
            def _(i):
                block = j * 2 + i
                products = []
                for s in range(2):
                    total = jnp.dot(table[s, 0, block], ub[s, 0], preferred_element_type=F32)
                    total += jnp.dot(table[s, 1, block], ub[s, 0], preferred_element_type=F32)
                    total += jnp.dot(table[s, 0, block], ub[s, 1], preferred_element_type=F32)
                    real = total[:TILE, :TILE] - total[TILE:, TILE:]
                    imag = total[:TILE, TILE:] + total[TILE:, :TILE]
                    products.append((real, imag))
                rows = pl.ds(pl.multiple_of(i * TILE, TILE), TILE)
                for part in range(2):
                    yy[p][part, 0, j, rows, :] = products[0][part] + products[1][part]
                    yy[p][part, 1, j, rows, :] = products[0][part] - products[1][part]

            for c in ((j, j + 2) if p == 0 else (0,) if j == 0 else ()):
                gather_points(p, c)

    @pl.loop(0, 4)
    def _(c):
        half = (zhi + 1 - c // 2) % 2
        j = c % 2
        take(yb.at[:, 0, 0, pl.ds(0, 248), :], ssem2.at[c])

        @pl.when(c < 3)
        def _():
            gather_points(1, c + 1)

        take(recv2.at[c], rsem2.at[c])
        point = lax.broadcasted_iota(jnp.int32, (8, TILE), 0)
        distance = (point + (half * HALF + q0 * 16 + j * 8)).astype(F32)
        radial_factor = 1.0 / (1.0 + 3.0 * distance / R) ** 2

        def to_lhs(cb, value):
            high, low = split(value)
            lhs[cb, :, 0:TILE] = high
            lhs[cb, :, TILE:2 * TILE] = low
            lhs[cb, :, 2 * TILE:] = high

        @pl.loop(0, CB)
        def _(cb):
            value = recv2[c, cb].reshape(TILE, TILE)
            adv[cb] = value
            to_lhs(cb, value)

        for degree in range(1, TAYLOR + 1):
            carried = jnp.zeros((TILE, TILE), F32)
            for position in range(NT):
                product = jnp.dot(
                    lhs[src[position]], tile_rhs[position], preferred_element_type=F32
                )
                scaled = product.reshape(16, 8, TILE) * rwb[half, j, wrow[position]][None]
                if position:
                    carried = jnp.where(same[position] == 1, carried, 0.0)
                carried = scaled.reshape(TILE, TILE) + carried
                sums[position + 1] = carried

            @pl.loop(0, CB)
            def _(cb):
                potential = sums[last[cb]].reshape(2, K, 8, TILE)
                strength = cpl[cb]
                rows = [
                    jnp.broadcast_to(strength[k:k + 1], (8, TILE)) * radial_factor
                    for k in range(K - 1)
                ]
                applied = []
                for part in range(2):
                    w = [recv2[c, cb, part, k] for k in range(K)]
                    for k in range(K):
                        value = potential[part, k]
                        if k + 1 < K:
                            value = value + rows[k] * w[k + 1]
                        if k > 0:
                            value = value + rows[k - 1] * w[k - 1]
                        applied.append(value)
                scale = 1.0 / degree
                term = [a * scale for a in applied[K:]] + [a * -scale for a in applied[:K]]
                if degree < TAYLOR:
                    stacked = jnp.concatenate(term, axis=0)
                    adv[cb] = adv[cb] + stacked
                    to_lhs(cb, stacked)
                    for i in range(2 * K):
                        recv2[c, cb, i // K, i % K] = term[i]
                else:
                    lanes = pl.ds(pl.multiple_of(cb * TILE, TILE), TILE)
                    for i in range(2 * K):
                        part, k = i // K, i % K
                        send3[c, k // 2, part, k % 2, :, lanes] = adv[cb, i * 8:(i + 1) * 8] + term[i]

        @pl.loop(0, 4)
        def _(o):
            pair = (zlo + o) % 4
            source = send3.at[c, pair]
            for jj in range(2):
                target = recv3[jj].at[z]
                own = jnp.logical_and(pair == zlo, c >= 2)

                @pl.when(jnp.logical_and(own, j == jj))
                def _():
                    pltpu.make_async_copy(source, target, rsem3.at[jj]).start()

                @pl.when(jnp.logical_and(jnp.logical_not(own), j == jj))
                def _():
                    pltpu.make_async_remote_copy(
                        source, target, ssem3.at[c], rsem3.at[jj],
                        device_id=(pair, half * 32 + q0), device_id_type=MESH,
                    ).start()

    for j in range(2):
        take(recv3[j], rsem3.at[j])
        for i in range(4):
            for cb in range(CB):
                for v in range(V):
                    res[i, cb, pl.ds(j * 64 + v, 8, stride=8), :] = recv3[j][
                        v, i // 2, i % 2, :, cb * TILE:(cb + 1) * TILE
                    ]
                pltpu.make_async_copy(
                    res.at[i, cb, pl.ds(j * 64, 64), :],
                    out_ref.at[i, pl.ds(j * 64, 64), pl.ds(cb * TILE, TILE)],
                    osem,
                ).start()

    take(res, osem)
    scattered(1, 0)
    scattered(1, 1)
    take(ya.at[:, :, :, pl.ds(0, 248), :], ssem2.at[4])
    for c in range(4):
        take(send3.at[c, pl.ds(0, 4 if c < 2 else 3)], ssem3.at[c])


def step(packet, radial_weight, tile_blocks, tile_list, coupling):
    flat = packet.reshape(4, 16 * V, CB * TILE)
    table = jnp.asarray(propagator_tables())
    anywhere = pl.BlockSpec(memory_space=pl.ANY)
    vmem = pl.BlockSpec(memory_space=pltpu.VMEM)
    dma = pltpu.SemaphoreType.DMA
    out = pl.pallas_call(
        kernel,
        out_shape=pltpu.VMEM(flat.shape, F32),
        in_specs=[
            anywhere, vmem, anywhere, pl.BlockSpec(memory_space=pltpu.SMEM), vmem, anywhere,
        ],
        out_specs=vmem,
        scratch_shapes=[
            pltpu.VMEM((4, CB, 128, TILE), F32),
            pltpu.VMEM((2, V, CB, 2, 16, TILE), F32),
            pltpu.VMEM((2, R, TILE), F32),
            pltpu.VMEM((2, R, TILE), F32),
            pltpu.VMEM((2, 2, HALF, 2 * TILE), BF16),
            pltpu.VMEM(table.shape, BF16),
            pltpu.VMEM((2, 2, 2, HALF // 2, TILE), F32),
            pltpu.VMEM((2, 2, 2, HALF // 2, TILE), F32),
            pltpu.VMEM((4, CB, 2, K, 8, TILE), F32),
            pltpu.VMEM((NT, TILE, TILE), F32),
            pltpu.VMEM((NT, 3 * TILE, TILE), BF16),
            pltpu.VMEM((CB, TILE, 3 * TILE), BF16),
            pltpu.VMEM((NT + 1, TILE, TILE), F32),
            pltpu.VMEM((CB, TILE, TILE), F32),
            pltpu.VMEM((2, Q, TILE), F32),
            pltpu.VMEM((2, 2, Q, 8, TILE), F32),
            pltpu.VMEM((CB, K, TILE), F32),
            pltpu.VMEM((4, 4, 2, 2, 8, CB * TILE), F32),
            pltpu.VMEM((8, 2, 2, 8, CB * TILE), F32),
            pltpu.VMEM((8, 2, 2, 8, CB * TILE), F32),
            pltpu.VMEM((4, CB, 128, TILE), F32),
            pltpu.SMEM((NT,), jnp.int32),
            pltpu.SMEM((NT,), jnp.int32),
            pltpu.SMEM((NT,), jnp.int32),
            pltpu.SMEM((NT,), jnp.int32),
            pltpu.SMEM((NT,), jnp.int32),
            pltpu.SMEM((CB,), jnp.int32),
            dma((4,)), dma(()), dma(()),
            dma((4,)), dma((2,)), dma((5,)), dma((4,)), dma((4,)), dma((2,)), dma((2,)), dma(()),
        ],
        compiler_params=pltpu.CompilerParams(
            collective_id=0, has_side_effects=True, vmem_limit_bytes=60 << 20
        ),
        name="wavepacket_step",
    )(flat, radial_weight, tile_blocks, tile_list.T, coupling, table)
    return out.reshape(packet.shape)


def solution(mesh):
    in_specs = (P(None, "hel", "rad"), P(None, "rad"), P(), P(), P())
    return jax.shard_map(
        step,
        mesh=mesh,
        in_specs=in_specs,
        out_specs=P(None, "hel", "rad"),
        check_vma=False,
    )
```
